32 devices in a mesh: row: 2 (over x), col: 16 (over z, y, core).
Axes of the slice: x: 2, y: 2, z: 4, core: 2. Of those that a mesh axis runs over, the one named last changes fastest.
Arguments:
- factors: bfloat16 [96, 256, 1024], P('col'), may hold values from -0.796875 to 0.796875
- metric_root: bfloat16 [1024, 1024], P('row'), may hold values from -1 to 2, as said below
- occ_energy: float32 [96], replicated, may hold values from -3 to -0.5
- vir_energy: float32 [256], replicated, may hold values from 0.2 to 4
- orbital_slot: int32 [96], replicated, may hold values from 0 to 95, each once
- source_plan: int32 [2, 2, 4], P('row'), may hold values from 0 to 95, as said below
- pair_list: int32 [2, 16, 2, 24], P('row', 'col'), may hold values from -1 to 23, as said below
Outputs:
- gamma_fit: float32 [2, 256, 8, 1024], P('row', 'col')
The draws below stay inside these ranges and needn't reach their ends.
Inputs may be any that keep to these rules, and one draw needn't show every extreme that they name: `metric_root`: Symmetric. `source_plan`: all entries are distinct orbitals. `pair_list`: each list holds 2 to 24 distinct codes k * 6 + l first and -1 in the remaining entries; in every draw some list is full.
All inputs are finite; a program needn't handle non-finite values.
Results may differ from the reference program's by a relative error of at most 0.003.
Values may be sent and summed in bfloat16 or wider, within the bound.
A program may use at most 128 MiB of HBM per device.

```python
import jax
import jax.numpy as jnp
from jax import lax

VIR = 256
NAUX = 1024
SRC = 4
STEPS = 2
OCC_DEV = 6
OCC = 96
N_ROW = 2
N_COL = 16


def draw_metric_root(key, part):
    key_noise, key_diagonal = jax.random.split(jax.random.fold_in(key, 7))
    noise = jax.random.normal(key_noise, (NAUX, NAUX), jnp.float32)
    symmetric = (noise + noise.T) * (0.3 / (2.0 * NAUX) ** 0.5)
    diagonal = jax.random.uniform(key_diagonal, (NAUX,), jnp.float32, 0.5, 1.5)
    return (symmetric + jnp.diag(diagonal)).astype(jnp.bfloat16)


def draw_source_plan(key, part):
    ordering = jax.random.permutation(jax.random.fold_in(key, 5), OCC)
    return ordering[:N_ROW * STEPS * SRC].reshape(N_ROW, STEPS, SRC).astype(jnp.int32)


def draw_pair_list(key, part):
    capacity = SRC * OCC_DEV
    lists = N_ROW * N_COL * STEPS
    key_first, key_second, key_full, key_order = jax.random.split(jax.random.fold_in(key, 11), 4)
    first_factor = jax.random.randint(key_first, (lists,), 0, capacity)
    second_factor = jax.random.randint(key_second, (lists,), 0, capacity + 1)
    counts = jnp.minimum(capacity, 2 + first_factor * second_factor // capacity)
    full_list = jax.random.randint(key_full, (), 0, lists)
    counts = jnp.where(jnp.arange(lists) == full_list, capacity, counts)
    order_keys = jax.random.split(key_order, lists)
    orders = jax.vmap(lambda single: jax.random.permutation(single, capacity))(order_keys)
    places = jnp.arange(capacity)
    entries = jnp.where(places[None, :] < counts[:, None], orders, -1)
    return entries.reshape(N_ROW, N_COL, STEPS, capacity).astype(jnp.int32)


def levels(key, dims, cuts, low, largest):
    def one(axis_at, parts):
        draws = jax.random.uniform(jax.random.fold_in(jax.random.fold_in(key, 6), axis_at), (parts,), jnp.float32, low / len(cuts), largest / len(cuts))
        return jnp.repeat(jnp.exp(draws), dims[axis_at] // parts).reshape((-1,) + (1,) * (len(dims) - axis_at - 1))

    level = one(*cuts[0])
    for cut in cuts[1:]:
        level = level * one(*cut)
    return level


def scatter_about(own_key, extent, scale, most, shards=(), held_as=jnp.bfloat16):
    factor_of = levels(own_key, extent, shards, -0.22, 0.18) if shards else 1.0
    result = jax.random.normal(own_key, extent, jnp.float32) * scale * factor_of
    return jnp.minimum(jnp.maximum(result, -most), most).astype(held_as)


def setup_inputs(seed: int = 0) -> dict:
    splits = jax.random.split(jax.random.key(seed), 8)
    factors = scatter_about(splits[0], (OCC, VIR, NAUX), (3.2 / NAUX ** 0.5), 0.796875, ((0, 16),))
    metric_root = draw_metric_root(jax.random.fold_in(splits[7], 71), 0)
    occ_energy = jnp.clip(jax.random.uniform(splits[2], (OCC,), jnp.float32, -3.0, -0.5), -3.0, -0.5)
    vir_energy = jnp.clip(jax.random.uniform(splits[3], (VIR,), jnp.float32, 0.2, 4.0), 0.2, 4.0)
    orbital_slot = jax.random.permutation(splits[4], OCC).astype(jnp.int32)
    source_plan = draw_source_plan(jax.random.fold_in(splits[7], 71), 0)
    pair_list = draw_pair_list(jax.random.fold_in(splits[7], 71), 0)
    return dict(factors=factors, metric_root=metric_root, occ_energy=occ_energy, vir_energy=vir_energy, orbital_slot=orbital_slot, source_plan=source_plan, pair_list=pair_list)


def pair_terms(sources, source_energy, local_factors, local_energy, virtual_energy, pair_mask):
    integrals = jnp.einsum('kaq,lbq->klab', sources.astype(jnp.float32), local_factors.astype(jnp.float32))
    denominator = (source_energy[:, None, None, None] + local_energy[None, :, None, None]
                   - virtual_energy[None, None, :, None] - virtual_energy[None, None, None, :])
    amplitude = integrals / denominator
    weights = ((2.0 * amplitude - jnp.swapaxes(amplitude, 2, 3)) * pair_mask[:, :, None, None]).astype(jnp.bfloat16)
    return jnp.einsum('klab,lbq->kaq', weights.astype(jnp.float32), local_factors.astype(jnp.float32))


def reference(factors, metric_root, occ_energy, vir_energy, orbital_slot, source_plan, pair_list):
    occupied = occ_energy.shape[0]
    slot_orbital = jnp.zeros((occupied,), jnp.int32).at[orbital_slot].set(jnp.arange(occupied, dtype=jnp.int32))
    code_range = jnp.arange(SRC * OCC_DEV, dtype=jnp.int32)

    def one_block(position):
        r = position // STEPS
        s = position % STEPS
        chosen = source_plan[r, s]
        sources = factors[orbital_slot[chosen]]
        source_energy = occ_energy[chosen]

        def add_column(running, c):
            first_slot = (c * OCC_DEV).astype(jnp.int32)
            local_factors = lax.dynamic_slice_in_dim(factors, first_slot, OCC_DEV, 0)
            local_energy = occ_energy[lax.dynamic_slice_in_dim(slot_orbital, first_slot, OCC_DEV, 0)]
            pair_codes = pair_list[r, c, s]
            pair_mask = jnp.any(pair_codes[:, None] == code_range[None, :], axis=0).reshape(SRC, OCC_DEV).astype(jnp.float32)
            return running + pair_terms(sources, source_energy, local_factors, local_energy, vir_energy, pair_mask), None

        running, unused = lax.scan(add_column, jnp.zeros((SRC, VIR, NAUX), jnp.float32), jnp.arange(N_COL, dtype=jnp.int32))
        gamma_rounded = running.astype(jnp.bfloat16)
        return jnp.dot(gamma_rounded.reshape(SRC * VIR, NAUX), metric_root, preferred_element_type=jnp.float32).reshape(SRC, VIR, NAUX)

    fitted = lax.map(one_block, jnp.arange(N_ROW * STEPS, dtype=jnp.int32))
    fitted = fitted.reshape(N_ROW, STEPS, SRC, VIR, NAUX).transpose(0, 3, 1, 2, 4)
    return fitted.reshape(N_ROW, VIR, STEPS * SRC, NAUX)
```

```python
from functools import partial

import jax
import jax.numpy as jnp
from jax import lax
from jax.experimental import pallas as pl
from jax.experimental.pallas import tpu as pltpu
from jax.sharding import PartitionSpec as P

MESH = pl.DeviceIdType.MESH
BF = jnp.bfloat16
F32 = jnp.float32

D_CORE, D_YRS, D_ZRS, D_ZAG, D_YAG, D_CAG, D_COMP = 0, 1, 2, 3, 4, 5, 6
D_GY, D_GZ, D_GEND = 7, 8, 9


def kernel(
    dims,
    pos_ref, flag_ref, esrc_ref, eloc_ref, mask_ref,
    f_ref, metric_ref, vcol_ref, vrow_ref,
    out_ref,
    own, c_in, t1, y_in, t2, z_in, full,
    wbuf, gsum, gc_out, gc_in, gmid, gy_out, gy_in, gz_out, gz_in, acc, mroot,
    s_c, r_c, s_y, r_y, s_z, r_z, s_za, r_za, s_ya, r_ya, s_ca, r_ca,
    s_gc, r_gc, s_gy, r_gy, s_gz, r_gz, s_m, r_m, l_m,
):
    K, A, B, NR, O, V, NP = dims
    HV = V // 2
    YV = HV // B
    ZP = NP // A
    R = V // (2 * A * B)
    row = lax.axis_index("row")
    col = lax.axis_index("col")
    h = lax.rem(col, 2)
    chip = col // 2
    y = lax.rem(chip, B)
    z = chip // B

    def at(zz, yy, hh):
        return (row, (zz * B + yy) * 2 + hh)

    partner = at(z, y, 1 - h)

    def ypeer(d):
        return lax.rem(y + d, B)

    def yfrom(d):
        return lax.rem(y + B - d, B)

    def zpeer(d):
        return lax.rem(z + d, A)

    def zfrom(d):
        return lax.rem(z + A - d, A)

    def rcopy(src, dst, ss, rs, dev):
        return pltpu.make_async_remote_copy(
            src_ref=src, dst_ref=dst, send_sem=ss, recv_sem=rs, device_id=dev, device_id_type=MESH
        )

    barrier = pltpu.get_barrier_semaphore()
    peers = [partner]
    peers += [at(z, ypeer(d), h) for d in range(1, B)]
    peers += [at(zpeer(d), y, h) for d in range(1, A)]
    peers += [(lax.rem(row + d, NR), col) for d in range(1, NR)]
    for dev in peers:
        pl.semaphore_signal(barrier, inc=1, device_id=dev, device_id_type=MESH)
    pl.semaphore_wait(barrier, len(peers))

    def m_copy(d):
        return rcopy(
            metric_ref, mroot.at[row], s_m.at[d - 1], r_m.at[d - 1], (lax.rem(row + d, NR), col)
        )

    m_local = pltpu.make_async_copy(metric_ref, mroot.at[row], l_m)
    m_local.start()

    hrow = pl.multiple_of(h * HV, HV)
    orow = pl.multiple_of((1 - h) * HV, HV)

    def lanes(zz):
        return pl.ds(pl.multiple_of(zz * ZP, ZP), ZP)

    def yrows(yy):
        return pl.ds(pl.multiple_of(yy * YV, YV), YV)

    def frows(yy):
        return pl.ds(pl.multiple_of(h * HV + yy * YV, YV), YV)

    def core_rs(k):
        return rcopy(own.at[k], c_in.at[k], s_c.at[k], r_c.at[k], partner)

    def y_rs(k, d):
        return rcopy(
            t1.at[k, yrows(ypeer(d))], y_in.at[k, d - 1], s_y.at[k, d - 1], r_y.at[k, d - 1],
            at(z, ypeer(d), h),
        )

    def z_rs(k, d):
        return rcopy(
            t2.at[k, :, lanes(zpeer(d))], z_in.at[k, d - 1], s_z.at[k, d - 1], r_z.at[k, d - 1],
            at(zpeer(d), y, h),
        )

    def z_ag(k, d):
        piece = full.at[k, frows(y), lanes(z)]
        return rcopy(piece, piece, s_za.at[k, d - 1], r_za.at[k, d - 1], at(zpeer(d), y, h))

    def z_ag_in(k, d):
        piece = full.at[k, frows(y), lanes(zfrom(d))]
        return rcopy(piece, piece, s_za.at[k, d - 1], r_za.at[k, d - 1], at(zpeer(d), y, h))

    def y_ag(k, d):
        piece = full.at[k, frows(y)]
        return rcopy(piece, piece, s_ya.at[k, d - 1], r_ya.at[k, d - 1], at(z, ypeer(d), h))

    def y_ag_in(k, d):
        piece = full.at[k, frows(yfrom(d))]
        return rcopy(piece, piece, s_ya.at[k, d - 1], r_ya.at[k, d - 1], at(z, ypeer(d), h))

    def c_ag(k):
        piece = full.at[k, pl.ds(hrow, HV)]
        return rcopy(piece, piece, s_ca.at[k], r_ca.at[k], partner)

    def c_ag_in(k):
        piece = full.at[k, pl.ds(orow, HV)]
        return rcopy(piece, piece, s_ca.at[k], r_ca.at[k], partner)

    def g_core(k):
        return rcopy(gc_out.at[k], gc_in.at[k], s_gc.at[k], r_gc.at[k], partner)

    def g_y(k, d):
        return rcopy(
            gy_out.at[k, d - 1], gy_in.at[k, d - 1], s_gy.at[k, d - 1], r_gy.at[k, d - 1],
            at(z, ypeer(d), h),
        )

    def g_z(k, d):
        return rcopy(
            gz_out.at[k, d - 1], gz_in.at[k, d - 1], s_gz.at[k, d - 1], r_gz.at[k, d - 1],
            at(zpeer(d), y, h),
        )

    def flagged(k, start):
        flag = jnp.full((HV, NP), flag_ref[k], F32).astype(BF)
        return f_ref[pos_ref[k], pl.ds(start, HV), :] * flag

    def st_core(k):
        own[k] = flagged(k, orow)
        core_rs(k).start()

    def st_yrs(k):
        core_rs(k).wait_recv()
        t1[k] = flagged(k, hrow) + c_in[k]
        for d in range(1, B):
            y_rs(k, d).start()

    def st_zrs(k):
        total = t1[k, yrows(y), :]
        for d in range(1, B):
            y_rs(k, d).wait_recv()
            total = total + y_in[k, d - 1]
        t2[k] = total
        for d in range(1, A):
            z_rs(k, d).start()

    def st_zag(k):
        total = t2[k, :, lanes(z)]
        for d in range(1, A):
            z_rs(k, d).wait_recv()
            total = total + z_in[k, d - 1]
        full[k, frows(y), lanes(z)] = total
        for d in range(1, A):
            z_ag(k, d).start()

    def st_yag(k):
        for d in range(1, A):
            z_ag_in(k, d).wait_recv()
        for d in range(1, B):
            y_ag(k, d).start()

    def st_cag(k):
        for d in range(1, B):
            y_ag_in(k, d).wait_recv()
        c_ag(k).start()

    def st_comp(k):
        c_ag_in(k).wait_recv()
        source = full[k]
        for l in range(O):
            ints = lax.dot_general(
                source, f_ref[l], (((1,), (1,)), ((), ())), preferred_element_type=F32
            )
            top = 2.0 * ints - jnp.transpose(ints)
            den = (esrc_ref[k] + eloc_ref[l] - vcol_ref[...]) - vrow_ref[...]
            wbuf[:, l * V:(l + 1) * V] = (top / den * mask_ref[k * O + l]).astype(BF)
        gamma = jnp.dot(
            wbuf[...], f_ref[...].reshape(O * V, NP), preferred_element_type=F32
        )
        gsum[k] = gamma.reshape(A, B, 2, R, NP)
        gc_out[k] = gsum[k, :, :, 1 - h].astype(BF)
        g_core(k).start()

    def st_gy(k):
        g_core(k).wait_recv()
        gmid[k] = gsum[k, :, :, h] + gc_in[k].astype(F32)
        for d in range(1, B):
            gy_out[k, d - 1] = gmid[k, :, ypeer(d)].astype(BF)
            g_y(k, d).start()

    def st_gz(k):
        for d in range(1, B):
            g_y(k, d).wait_recv()
            gmid[k, :, y] = gmid[k, :, y] + gy_in[k, d - 1].astype(F32)
        for d in range(1, A):
            gz_out[k, d - 1] = gmid[k, zpeer(d), y].astype(BF)
            g_z(k, d).start()

    def st_gend(k):
        total = gmid[k, z, y]
        for d in range(1, A):
            g_z(k, d).wait_recv()
            total = total + gz_in[k, d - 1].astype(F32)
        acc[k] = total

    stages = (
        (D_CORE, st_core), (D_YRS, st_yrs), (D_ZRS, st_zrs), (D_ZAG, st_zag), (D_YAG, st_yag),
        (D_CAG, st_cag), (D_GEND, st_gend), (D_GZ, st_gz), (D_GY, st_gy), (D_COMP, st_comp),
    )

    def tick(t, carry):
        for delay, stage in stages:
            k = t - delay
            pl.when((k >= 0) & (k < K))(partial(stage, k))

        @pl.when(t == 2)
        def _():
            for d in range(1, NR):
                m_copy(d).start()

        return carry

    lax.fori_loop(0, K + D_GEND, tick, 0)

    m_local.wait()
    for d in range(1, NR):
        m_copy(d).wait()
    root = mroot[...].reshape(NP, NP)
    gamma = acc[...].reshape(K * R, NP)
    high = gamma.astype(BF)
    low = (gamma - high.astype(F32)).astype(BF)
    fitted = jnp.dot(high, root, preferred_element_type=F32)
    fitted = fitted + jnp.dot(low, root, preferred_element_type=F32)
    out_ref[...] = fitted.reshape(K, R, NP)

    def drain(k, carry):
        core_rs(k).wait_send()
        for d in range(1, B):
            y_rs(k, d).wait_send()
            y_ag(k, d).wait_send()
            g_y(k, d).wait_send()
        for d in range(1, A):
            z_rs(k, d).wait_send()
            z_ag(k, d).wait_send()
            g_z(k, d).wait_send()
        c_ag(k).wait_send()
        g_core(k).wait_send()
        return carry

    lax.fori_loop(0, K, drain, 0)


def on_device(factors, metric_root, occ_energy, vir_energy, orbital_slot, source_plan, pair_list):
    O, V, NP = factors.shape
    n = lax.axis_size("col")
    NR = lax.axis_size("row")
    chips = n // 2
    A = 4 if chips % 4 == 0 else chips
    B = chips // A
    steps, sources = source_plan.shape[1:]
    K = steps * sources
    R = V // n
    HV, YV, ZP = V // 2, V // 2 // B, NP // A
    column = lax.axis_index("col")
    occupied = occ_energy.shape[0]
    local_slots = column * O + jnp.arange(O, dtype=jnp.int32)
    local_match = orbital_slot[None, :] == local_slots[:, None]
    local_energy = jnp.sum(jnp.where(local_match, occ_energy[None, :], 0.0), axis=1)
    plan = source_plan.reshape(K)
    source_match = plan[:, None] == jnp.arange(occupied, dtype=jnp.int32)[None, :]
    source_energy = jnp.sum(jnp.where(source_match, occ_energy[None, :], 0.0), axis=1)
    source_slot = jnp.sum(jnp.where(source_match, orbital_slot[None, :], 0), axis=1)
    position = (source_slot % O).astype(jnp.int32)
    flag = (source_slot // O == column).astype(F32)
    codes = jnp.arange(sources * O, dtype=jnp.int32)
    pair_mask = jnp.any(
        pair_list.reshape(steps, -1)[:, :, None] == codes[None, None, :], axis=1
    ).astype(F32).reshape(K * O)

    dma = pltpu.SemaphoreType.DMA
    b1, a1 = max(B - 1, 1), max(A - 1, 1)
    per_k = (K,)
    sems = []
    for shape in (per_k, (K, b1), (K, a1), (K, a1), (K, b1), per_k, per_k, (K, b1), (K, a1)):
        sems += [dma(shape), dma(shape)]
    nr1 = max(NR - 1, 1)
    sems += [dma((nr1,)), dma((nr1,)), dma]
    vm = pltpu.VMEM
    out = pl.pallas_call(
        partial(kernel, (K, A, B, NR, O, V, NP)),
        out_shape=jax.ShapeDtypeStruct((K, R, NP), F32),
        in_specs=[pl.BlockSpec(memory_space=pltpu.SMEM)] * 5 + [pl.BlockSpec(memory_space=vm)] * 4,
        out_specs=pl.BlockSpec(memory_space=vm),
        scratch_shapes=[
            vm((K, HV, NP), BF),
            vm((K, HV, NP), BF),
            vm((K, HV, NP), BF),
            vm((K, b1, YV, NP), BF),
            vm((K, YV, NP), BF),
            vm((K, a1, YV, ZP), BF),
            vm((K, V, NP), BF),
            vm((V, O * V), BF),
            vm((K, A, B, 2, R, NP), F32),
            vm((K, A, B, R, NP), BF),
            vm((K, A, B, R, NP), BF),
            vm((K, A, B, R, NP), F32),
            vm((K, b1, A, R, NP), BF),
            vm((K, b1, A, R, NP), BF),
            vm((K, a1, R, NP), BF),
            vm((K, a1, R, NP), BF),
            vm((K, R, NP), F32),
            vm((NR, NP // NR, NP), BF),
        ] + sems,
        compiler_params=pltpu.CompilerParams(
            collective_id=0, has_side_effects=True, vmem_limit_bytes=60 * 1024 * 1024
        ),
    )(
        position, flag, source_energy, local_energy, pair_mask,
        factors, metric_root, vir_energy[:, None], vir_energy[None, :],
    )
    return jnp.transpose(out, (1, 0, 2))[None]


def solution(mesh):
    in_specs = (
        P("col", None, None),
        P("row", None),
        P(),
        P(),
        P(),
        P("row", None, None),
        P("row", "col", None, None),
    )
    out_specs = P("row", "col", None, None)
    return jax.shard_map(
        on_device, mesh=mesh, in_specs=in_specs, out_specs=out_specs, check_vma=False
    )
```

```python
from functools import partial

import jax
import jax.numpy as jnp
from jax import lax
from jax.experimental import pallas as pl
from jax.experimental.pallas import tpu as pltpu
from jax.sharding import PartitionSpec as P

MESH = pl.DeviceIdType.MESH
BF = jnp.bfloat16
F32 = jnp.float32

def kernel(
    dims,
    plan_ref, slot_ref, occ_ref,
    f_ref, metric_ref, vrow_ref, slots_ref, occs_ref, pairs_ref,
    out_ref,
    own, c_in, t1, y_in, t2, rin, rout, lin, lout, zr_in, zr_out, zl_in, zl_out, zy_out, zy_in, full,
    vsum, eloc,
    wbuf, gsum, gc_out, gc_in, gmid, gy_out, gy_in, gz_out, gz_in, acc, mroot,
    s_c, r_c, s_y, r_y, s_r, r_r, s_l, r_l, s_zr, r_zr, s_zl, r_zl, s_zy, r_zy, s_ar, r_ar, s_al, r_al,
    s_ya, r_ya, s_ca, r_ca,
    s_gc, r_gc, s_gy, r_gy, s_gz, r_gz, s_m, r_m, l_m,
):
    K, A, B, NR, O, V, NP, SRC = dims
    HV = V // 2
    YV = HV // B
    ZP = NP // A
    R = V // (2 * A * B)
    row = lax.axis_index("row")
    col = lax.axis_index("col")
    h = lax.rem(col, 2)
    chip = col // 2
    y = lax.rem(chip, B)
    z = chip // B

    def at(zz, yy, hh):
        return (row, (zz * B + yy) * 2 + hh)

    partner = at(z, y, 1 - h)

    def ypeer(d):
        return lax.rem(y + d, B)

    def yfrom(d):
        return lax.rem(y + B - d, B)

    def zpeer(d):
        return lax.rem(z + d, A)

    def zfrom(d):
        return lax.rem(z + A - d, A)

    def rcopy(src, dst, ss, rs, dev):
        return pltpu.make_async_remote_copy(
            src_ref=src, dst_ref=dst, send_sem=ss, recv_sem=rs, device_id=dev, device_id_type=MESH
        )

    barrier = pltpu.get_barrier_semaphore()
    peers = [partner]
    peers += [at(z, ypeer(d), h) for d in range(1, B)]
    peers += [at(zpeer(d), y, h) for d in range(1, A)]
    peers += [(lax.rem(row + d, NR), col) for d in range(1, NR)]
    for dev in peers:
        pl.semaphore_signal(barrier, inc=1, device_id=dev, device_id_type=MESH)
    pl.semaphore_wait(barrier, len(peers))

    def m_copy(d):
        return rcopy(
            metric_ref, mroot.at[row], s_m.at[d - 1], r_m.at[d - 1], (lax.rem(row + d, NR), col)
        )

    m_local = pltpu.make_async_copy(metric_ref, mroot.at[row], l_m)
    m_local.start()

    hrow = pl.multiple_of(h * HV, HV)
    orow = pl.multiple_of((1 - h) * HV, HV)

    def lanes(zz):
        return pl.ds(pl.multiple_of(zz * ZP, ZP), ZP)

    def yrows(yy):
        return pl.ds(pl.multiple_of(yy * YV, YV), YV)

    def frows(yy):
        return pl.ds(pl.multiple_of(h * HV + yy * YV, YV), YV)

    def core_rs(k):
        return rcopy(own.at[k], c_in.at[k], s_c.at[k], r_c.at[k], partner)

    def y_rs(k, d):
        return rcopy(
            t1.at[k, yrows(ypeer(d))], y_in.at[k, d - 1], s_y.at[k, d - 1], r_y.at[k, d - 1],
            at(z, ypeer(d), h),
        )

    right, left = at(lax.rem(z + 1, A), y, h), at(lax.rem(z + A - 1, A), y, h)

    def sweep_r(k):
        return rcopy(rout.at[k], rin.at[k], s_r.at[k], r_r.at[k], right)

    def sweep_l(k):
        return rcopy(lout.at[k], lin.at[k], s_l.at[k], r_l.at[k], left)

    def chain_r(k, d):
        cut = pl.ds(d * ZP, ZP)
        return rcopy(
            zr_out.at[k, :, cut], zr_in.at[k, :, cut], s_zr.at[k, d], r_zr.at[k, d], right
        )

    def chain_l(k, d):
        cut = pl.ds(d * ZP, ZP)
        return rcopy(
            zl_out.at[k, :, cut], zl_in.at[k, :, cut], s_zl.at[k, d], r_zl.at[k, d], left
        )

    def z_y(k, d):
        return rcopy(
            zy_out.at[k], zy_in.at[k, d - 1], s_zy.at[k, d - 1], r_zy.at[k, d - 1],
            at(z, ypeer(d), h),
        )

    def gather_r(k, j, zz):
        piece = full.at[k, pl.ds(hrow, HV), lanes(zz)]
        return rcopy(piece, piece, s_ar.at[k, j - 1], r_ar.at[k, j - 1], right)

    def gather_l(k, j, zz):
        piece = full.at[k, pl.ds(hrow, HV), lanes(zz)]
        return rcopy(piece, piece, s_al.at[k, j - 1], r_al.at[k, j - 1], left)

    def y_ag(k, d):
        piece = full.at[k, frows(y)]
        return rcopy(piece, piece, s_ya.at[k, d - 1], r_ya.at[k, d - 1], at(z, ypeer(d), h))

    def y_ag_in(k, d):
        piece = full.at[k, frows(yfrom(d))]
        return rcopy(piece, piece, s_ya.at[k, d - 1], r_ya.at[k, d - 1], at(z, ypeer(d), h))

    def c_ag(k):
        piece = full.at[k, pl.ds(hrow, HV)]
        return rcopy(piece, piece, s_ca.at[k], r_ca.at[k], partner)

    def c_ag_in(k):
        piece = full.at[k, pl.ds(orow, HV)]
        return rcopy(piece, piece, s_ca.at[k], r_ca.at[k], partner)

    def g_core(k):
        return rcopy(gc_out.at[k], gc_in.at[k], s_gc.at[k], r_gc.at[k], partner)

    def g_y(k, d):
        return rcopy(
            gy_out.at[k, d - 1], gy_in.at[k, d - 1], s_gy.at[k, d - 1], r_gy.at[k, d - 1],
            at(z, ypeer(d), h),
        )

    def g_z(k, d):
        return rcopy(
            gz_out.at[k, d - 1], gz_in.at[k, d - 1], s_gz.at[k, d - 1], r_gz.at[k, d - 1],
            at(zpeer(d), y, h),
        )

    def flagged(k, start):
        slot = slot_ref[plan_ref[k]]
        flag = jnp.where(slot // O == col, jnp.float32(1.0), jnp.float32(0.0))
        return f_ref[slot % O, pl.ds(start, HV), :] * jnp.full((HV, NP), flag, F32).astype(BF)

    def st_core(k):
        own[k] = flagged(k, orow)
        core_rs(k).start()

    def st_half(k):
        core_rs(k).wait_recv()
        t1[k] = flagged(k, hrow) + c_in[k]

    def y_send(k):
        for d in range(1, B):
            y_rs(k, d).start()

    def y_sum(k):
        total = t1[k, yrows(y), :]
        for d in range(1, B):
            y_rs(k, d).wait_recv()
            total = total + y_in[k, d - 1]
        t2[k] = total

    def st_sweep_r(k):
        @pl.when(z == 0)
        def _():
            rout[k] = t2[k]

        @pl.when((z > 0) & (z < A - 1))
        def _():
            sweep_r(k).wait_recv()
            rout[k] = t2[k] + rin[k]

        @pl.when(z < A - 1)
        def _():
            sweep_r(k).start()

    def st_sweep_l(k):
        @pl.when(z == A - 1)
        def _():
            lout[k] = t2[k]

        @pl.when((z > 0) & (z < A - 1))
        def _():
            sweep_l(k).wait_recv()
            lout[k] = t2[k] + lin[k]

        @pl.when(z > 0)
        def _():
            sweep_l(k).start()

    def st_yag(k):
        @pl.when(z == 0)
        def _():
            sweep_l(k).wait_recv()
            full[k, frows(y), :] = t2[k] + lin[k]

        @pl.when(z == A - 1)
        def _():
            sweep_r(k).wait_recv()
            full[k, frows(y), :] = t2[k] + rin[k]

        @pl.when((z > 0) & (z < A - 1))
        def _():
            full[k, frows(y), :] = rout[k] + lin[k]

        for d in range(1, B):
            y_ag(k, d).start()

    def st_cag(k):
        for d in range(1, B):
            y_ag_in(k, d).wait_recv()
        c_ag(k).start()

    def st_chain_r(k):
        for d in range(1, A):
            cut = slice(d * ZP, (d + 1) * ZP)

            @pl.when((z < d) & (z == 0))
            def _():
                zr_out[k, :, cut] = t1[k, :, cut]

            @pl.when((z < d) & (z > 0))
            def _():
                chain_r(k, d).wait_recv()
                zr_out[k, :, cut] = t1[k, :, cut] + zr_in[k, :, cut]

            @pl.when(z < d)
            def _():
                chain_r(k, d).start()

    def st_chain_l(k):
        for d in range(A - 1):
            cut = slice(d * ZP, (d + 1) * ZP)

            @pl.when((z > d) & (z == A - 1))
            def _():
                zl_out[k, :, cut] = t1[k, :, cut]

            @pl.when((z > d) & (z < A - 1))
            def _():
                chain_l(k, d).wait_recv()
                zl_out[k, :, cut] = t1[k, :, cut] + zl_in[k, :, cut]

            @pl.when(z > d)
            def _():
                chain_l(k, d).start()

    def st_zy(k):
        for d in range(A):
            cut = slice(d * ZP, (d + 1) * ZP)

            @pl.when(z == d)
            def _():
                total = t1[k, :, cut]
                if d > 0:
                    chain_r(k, d).wait_recv()
                    total = total + zr_in[k, :, cut]
                if d < A - 1:
                    chain_l(k, d).wait_recv()
                    total = total + zl_in[k, :, cut]
                zy_out[k] = total

        for d in range(1, B):
            z_y(k, d).start()

    def st_zysum(k):
        total = zy_out[k]
        for d in range(1, B):
            z_y(k, d).wait_recv()
            total = total + zy_in[k, d - 1]
        full[k, pl.ds(hrow, HV), lanes(z)] = total

    def gather_in(k, j):
        @pl.when(z - j >= 0)
        def _():
            gather_r(k, j, lax.rem(z - j + A, A)).wait_recv()

        @pl.when(z + j < A)
        def _():
            gather_l(k, j, lax.rem(z + j, A)).wait_recv()

    def gather_out(k, j):
        @pl.when((z - j + 1 >= 0) & (z < A - 1))
        def _():
            gather_r(k, j, lax.rem(z - j + 1 + A, A)).start()

        @pl.when((z + j - 1 < A) & (z > 0))
        def _():
            gather_l(k, j, lax.rem(z + j - 1, A)).start()

    def st_gather(j, k):
        if j > 1:
            gather_in(k, j - 1)
        gather_out(k, j)

    def st_zcag(k):
        gather_in(k, A - 1)
        c_ag(k).start()

    def st_comp(k):
        c_ag_in(k).wait_recv()
        source = full[k]
        for l in range(O):
            ints = lax.dot_general(
                source, f_ref[l], (((1,), (1,)), ((), ())), preferred_element_type=F32
            )
            top = 2.0 * ints - jnp.transpose(ints)
            den = (occ_ref[plan_ref[k]] + eloc[l][:, :1]) - vsum[...]
            code = lax.rem(k, SRC) * O + l
            hits = jnp.where(pairs_ref[pl.ds(k // SRC, 1), :] == code, 1.0, 0.0)
            listed = jnp.max(hits, axis=1, keepdims=True)
            wbuf[:, l * V:(l + 1) * V] = (top / den * listed).astype(BF)
        gamma = jnp.dot(
            wbuf[...], f_ref[...].reshape(O * V, NP), preferred_element_type=F32
        )
        gsum[k] = gamma.reshape(A, B, 2, R, NP)
        gc_out[k] = gsum[k, :, :, 1 - h].astype(BF)
        g_core(k).start()

    def st_gy(k):
        g_core(k).wait_recv()
        gmid[k] = gsum[k, :, :, h] + gc_in[k].astype(F32)
        for d in range(1, B):
            gy_out[k, d - 1] = gmid[k, :, ypeer(d)].astype(BF)
            g_y(k, d).start()

    def st_gz(k):
        for d in range(1, B):
            g_y(k, d).wait_recv()
            gmid[k, :, y] = gmid[k, :, y] + gy_in[k, d - 1].astype(F32)
        for d in range(1, A):
            gz_out[k, d - 1] = gmid[k, zpeer(d), y].astype(BF)
            g_z(k, d).start()

    def st_gend(k):
        total = gmid[k, z, y]
        for d in range(1, A):
            g_z(k, d).wait_recv()
            total = total + gz_in[k, d - 1].astype(F32)
        acc[k] = total

    def z_first(k):
        return (lax.rem(k, 2) == 1) & (k + 2 < K)

    vrow = jnp.broadcast_to(vrow_ref[...], (V, V))
    vsum[...] = vrow + jnp.transpose(vrow)
    for l in range(O):
        mine = jnp.where(slots_ref[...] == col * O + l, occs_ref[...], 0.0)
        eloc[l] = jnp.broadcast_to(jnp.sum(mine, axis=1, keepdims=True), (1, 128))

    def tick(t, carry):
        def run(delay, stage, kind):
            k = t - delay
            kept = (k >= 0) & (k < K)
            if kind == "z":
                kept = kept & z_first(k)
            if kind == "y":
                kept = kept & jnp.logical_not(z_first(k))
            pl.when(kept)(partial(stage, k))

        mirror = A - 1 - z
        run(0, st_core, "")
        run(1, st_half, "")
        run(1, y_send, "y")
        run(1 + z, st_chain_r, "z")
        run(1 + mirror, st_chain_l, "z")
        run(2, y_sum, "y")
        run(2 + z, st_sweep_r, "y")
        run(2 + mirror, st_sweep_l, "y")
        run(A, st_zy, "z")
        run(A + 1, st_yag, "y")
        run(A + 1, st_zysum, "z")
        for j in range(1, A):
            run(A + j, partial(st_gather, j), "z")
        run(2 * A, st_zcag, "z")
        run(A + 2, st_cag, "y")
        y_comp, z_comp = A + 3, 2 * A + 1
        for comp, kind in ((y_comp, "y"), (z_comp, "z")):
            run(comp + 3, st_gend, kind)
            run(comp + 2, st_gz, kind)
            run(comp + 1, st_gy, kind)
            run(comp, st_comp, kind)

        @pl.when(t == 2)
        def _():
            for d in range(1, NR):
                m_copy(d).start()

        return carry

    lax.fori_loop(0, K + 2 * A + 4, tick, 0)

    m_local.wait()
    for d in range(1, NR):
        m_copy(d).wait()
    root = mroot[...].reshape(NP, NP)
    gamma = acc[...].reshape(K * R, NP)
    high = gamma.astype(BF)
    low = (gamma - high.astype(F32)).astype(BF)
    fitted = jnp.dot(high, root, preferred_element_type=F32)
    fitted = fitted + jnp.dot(low, root, preferred_element_type=F32)
    out_ref[...] = fitted.reshape(K, R, NP)

    def drain(k, carry):
        core_rs(k).wait_send()
        for d in range(1, B):
            g_y(k, d).wait_send()
        for d in range(1, A):
            g_z(k, d).wait_send()
        c_ag(k).wait_send()
        g_core(k).wait_send()

        @pl.when(jnp.logical_not(z_first(k)))
        def _():
            for d in range(1, B):
                y_rs(k, d).wait_send()
                y_ag(k, d).wait_send()
            pl.when(z < A - 1)(lambda: sweep_r(k).wait_send())
            pl.when(z > 0)(lambda: sweep_l(k).wait_send())

        @pl.when(z_first(k))
        def _():
            for d in range(1, B):
                z_y(k, d).wait_send()
            for d in range(A):
                pl.when(z < d)(lambda: chain_r(k, d).wait_send())
                pl.when(z > d)(lambda: chain_l(k, d).wait_send())
            for j in range(1, A):
                pl.when((z - j + 1 >= 0) & (z < A - 1))(
                    lambda: gather_r(k, j, lax.rem(z - j + 1 + A, A)).wait_send()
                )
                pl.when((z + j - 1 < A) & (z > 0))(
                    lambda: gather_l(k, j, lax.rem(z + j - 1, A)).wait_send()
                )

        return carry

    lax.fori_loop(0, K, drain, 0)


def on_device(factors, metric_root, occ_energy, vir_energy, orbital_slot, source_plan, pair_list):
    O, V, NP = factors.shape
    n = lax.axis_size("col")
    NR = lax.axis_size("row")
    chips = n // 2
    A = 4 if chips % 4 == 0 else chips
    B = chips // A
    steps, sources = source_plan.shape[1:]
    K = steps * sources
    R = V // n
    HV, YV, ZP = V // 2, V // 2 // B, NP // A
    dma = pltpu.SemaphoreType.DMA
    b1, a1 = max(B - 1, 1), max(A - 1, 1)
    per_k = (K,)
    sems = []
    for shape in (
        per_k, (K, b1), per_k, per_k, (K, A), (K, A), (K, b1), (K, a1), (K, a1),
        (K, b1), per_k, per_k, (K, b1), (K, a1),
    ):
        sems += [dma(shape), dma(shape)]
    nr1 = max(NR - 1, 1)
    sems += [dma((nr1,)), dma((nr1,)), dma]
    vm = pltpu.VMEM
    out = pl.pallas_call(
        partial(kernel, (K, A, B, NR, O, V, NP, sources)),
        out_shape=jax.ShapeDtypeStruct((K, R, NP), F32),
        in_specs=[pl.BlockSpec(memory_space=pltpu.SMEM)] * 3 + [pl.BlockSpec(memory_space=vm)] * 6,
        out_specs=pl.BlockSpec(memory_space=vm),
        scratch_shapes=[
            vm((K, HV, NP), BF),
            vm((K, HV, NP), BF),
            vm((K, HV, NP), BF),
            vm((K, b1, YV, NP), BF),
            vm((K, YV, NP), BF),
            vm((K, YV, NP), BF),
            vm((K, YV, NP), BF),
            vm((K, YV, NP), BF),
            vm((K, YV, NP), BF),
            vm((K, HV, NP), BF),
            vm((K, HV, NP), BF),
            vm((K, HV, NP), BF),
            vm((K, HV, NP), BF),
            vm((K, HV, ZP), BF),
            vm((K, b1, HV, ZP), BF),
            vm((K, V, NP), BF),
            vm((V, V), F32),
            vm((O, 1, 128), F32),
            vm((V, O * V), BF),
            vm((K, A, B, 2, R, NP), F32),
            vm((K, A, B, R, NP), BF),
            vm((K, A, B, R, NP), BF),
            vm((K, A, B, R, NP), F32),
            vm((K, b1, A, R, NP), BF),
            vm((K, b1, A, R, NP), BF),
            vm((K, a1, R, NP), BF),
            vm((K, a1, R, NP), BF),
            vm((K, R, NP), F32),
            vm((NR, NP // NR, NP), BF),
        ] + sems,
        compiler_params=pltpu.CompilerParams(
            collective_id=0, has_side_effects=True, vmem_limit_bytes=60 * 1024 * 1024
        ),
    )(
        source_plan.reshape(K), orbital_slot, occ_energy,
        factors, metric_root, vir_energy[None, :], orbital_slot[None, :], occ_energy[None, :],
        pair_list.reshape(steps, -1),
    )
    return jnp.transpose(out, (1, 0, 2))[None]


def solution(mesh):
    in_specs = (
        P("col", None, None),
        P("row", None),
        P(),
        P(),
        P(),
        P("row", None, None),
        P("row", "col", None, None),
    )
    out_specs = P("row", "col", None, None)
    return jax.shard_map(
        on_device, mesh=mesh, in_specs=in_specs, out_specs=out_specs, check_vma=False
    )
```

```python
from functools import partial

import jax
import jax.numpy as jnp
from jax import lax
from jax.experimental import pallas as pl
from jax.experimental.pallas import tpu as pltpu
from jax.sharding import PartitionSpec as P

MESH = pl.DeviceIdType.MESH
BF = jnp.bfloat16
F32 = jnp.float32

def kernel(
    dims,
    plan_ref, slot_ref, occ_ref,
    f_ref, metric_ref, vrow_ref, slots_ref, occs_ref, pairs_ref,
    out_ref,
    own, c_in, t1, y_in, t2, rin, rout, lin, lout, zr_in, zr_out, zl_in, zl_out, zy_out, zy_in, full,
    vsum, eloc,
    wbuf, gsum, gc_out, gc_in, gmid, gy_out, gy_in, gz_out, gz_in, acc, mroot,
    s_c, r_c, s_y, r_y, s_r, r_r, s_l, r_l, s_zr, r_zr, s_zl, r_zl, s_zy, r_zy, s_ar, r_ar, s_al, r_al,
    s_ya, r_ya, s_ca, r_ca,
    s_gc, r_gc, s_gy, r_gy, s_gz, r_gz, s_m, r_m, l_m,
):
    K, A, B, NR, O, V, NP, SRC = dims
    HV = V // 2
    YV = HV // B
    ZP = NP // A
    R = V // (2 * A * B)
    row = lax.axis_index("row")
    col = lax.axis_index("col")
    h = lax.rem(col, 2)
    chip = col // 2
    y = lax.rem(chip, B)
    z = chip // B

    def at(zz, yy, hh):
        return (row, (zz * B + yy) * 2 + hh)

    partner = at(z, y, 1 - h)

    def ypeer(d):
        return lax.rem(y + d, B)

    def yfrom(d):
        return lax.rem(y + B - d, B)

    def zpeer(d):
        return lax.rem(z + d, A)

    def zfrom(d):
        return lax.rem(z + A - d, A)

    def rcopy(src, dst, ss, rs, dev):
        return pltpu.make_async_remote_copy(
            src_ref=src, dst_ref=dst, send_sem=ss, recv_sem=rs, device_id=dev, device_id_type=MESH
        )

    barrier = pltpu.get_barrier_semaphore()
    peers = [partner]
    peers += [at(z, ypeer(d), h) for d in range(1, B)]
    peers += [at(zpeer(d), y, h) for d in range(1, A)]
    peers += [(lax.rem(row + d, NR), col) for d in range(1, NR)]
    for dev in peers:
        pl.semaphore_signal(barrier, inc=1, device_id=dev, device_id_type=MESH)
    pl.semaphore_wait(barrier, len(peers))

    def m_copy(d):
        return rcopy(
            metric_ref, mroot.at[row], s_m.at[d - 1], r_m.at[d - 1], (lax.rem(row + d, NR), col)
        )

    m_local = pltpu.make_async_copy(metric_ref, mroot.at[row], l_m)
    m_local.start()

    hrow = pl.multiple_of(h * HV, HV)
    orow = pl.multiple_of((1 - h) * HV, HV)

    def lanes(zz):
        return pl.ds(pl.multiple_of(zz * ZP, ZP), ZP)

    def yrows(yy):
        return pl.ds(pl.multiple_of(yy * YV, YV), YV)

    def frows(yy):
        return pl.ds(pl.multiple_of(h * HV + yy * YV, YV), YV)

    def core_rs(k):
        return rcopy(own.at[k], c_in.at[k], s_c.at[k], r_c.at[k], partner)

    def y_rs(k, d):
        return rcopy(
            t1.at[k, yrows(ypeer(d))], y_in.at[k, d - 1], s_y.at[k, d - 1], r_y.at[k, d - 1],
            at(z, ypeer(d), h),
        )

    right, left = at(lax.rem(z + 1, A), y, h), at(lax.rem(z + A - 1, A), y, h)

    def sweep_r(k):
        return rcopy(rout.at[k], rin.at[k], s_r.at[k], r_r.at[k], right)

    def sweep_l(k):
        return rcopy(lout.at[k], lin.at[k], s_l.at[k], r_l.at[k], left)

    def chain_r(k, d):
        cut = pl.ds(d * ZP, ZP)
        return rcopy(
            zr_out.at[k, :, cut], zr_in.at[k, :, cut], s_zr.at[k, d], r_zr.at[k, d], right
        )

    def chain_l(k, d):
        cut = pl.ds(d * ZP, ZP)
        return rcopy(
            zl_out.at[k, :, cut], zl_in.at[k, :, cut], s_zl.at[k, d], r_zl.at[k, d], left
        )

    def z_y(k, d):
        return rcopy(
            zy_out.at[k], zy_in.at[k, d - 1], s_zy.at[k, d - 1], r_zy.at[k, d - 1],
            at(z, ypeer(d), h),
        )

    def gather_r(k, j, zz):
        piece = full.at[k, pl.ds(hrow, HV), lanes(zz)]
        return rcopy(piece, piece, s_ar.at[k, j - 1], r_ar.at[k, j - 1], right)

    def gather_l(k, j, zz):
        piece = full.at[k, pl.ds(hrow, HV), lanes(zz)]
        return rcopy(piece, piece, s_al.at[k, j - 1], r_al.at[k, j - 1], left)

    def y_ag(k, d):
        piece = full.at[k, frows(y)]
        return rcopy(piece, piece, s_ya.at[k, d - 1], r_ya.at[k, d - 1], at(z, ypeer(d), h))

    def y_ag_in(k, d):
        piece = full.at[k, frows(yfrom(d))]
        return rcopy(piece, piece, s_ya.at[k, d - 1], r_ya.at[k, d - 1], at(z, ypeer(d), h))

    def c_ag(k):
        piece = full.at[k, pl.ds(hrow, HV)]
        return rcopy(piece, piece, s_ca.at[k], r_ca.at[k], partner)

    def c_ag_in(k):
        piece = full.at[k, pl.ds(orow, HV)]
        return rcopy(piece, piece, s_ca.at[k], r_ca.at[k], partner)

    def g_core(k):
        return rcopy(gc_out.at[k], gc_in.at[k], s_gc.at[k], r_gc.at[k], partner)

    def g_y(k, d):
        return rcopy(
            gy_out.at[k, d - 1], gy_in.at[k, d - 1], s_gy.at[k, d - 1], r_gy.at[k, d - 1],
            at(z, ypeer(d), h),
        )

    def g_z(k, d):
        return rcopy(
            gz_out.at[k, d - 1], gz_in.at[k, d - 1], s_gz.at[k, d - 1], r_gz.at[k, d - 1],
            at(zpeer(d), y, h),
        )

    def flagged(k, start):
        slot = slot_ref[plan_ref[k]]
        flag = jnp.where(slot // O == col, jnp.float32(1.0), jnp.float32(0.0))
        return f_ref[slot % O, pl.ds(start, HV), :] * jnp.full((HV, NP), flag, F32).astype(BF)

    def st_core(k):
        own[k] = flagged(k, orow)
        core_rs(k).start()

    def st_half(k):
        core_rs(k).wait_recv()
        t1[k] = flagged(k, hrow) + c_in[k]

    def y_send(k):
        for d in range(1, B):
            y_rs(k, d).start()

    def y_sum(k):
        total = t1[k, yrows(y), :]
        for d in range(1, B):
            y_rs(k, d).wait_recv()
            total = total + y_in[k, d - 1]
        t2[k] = total

    def st_sweep_r(k):
        @pl.when(z == 0)
        def _():
            rout[k] = t2[k]

        @pl.when((z > 0) & (z < A - 1))
        def _():
            sweep_r(k).wait_recv()
            rout[k] = t2[k] + rin[k]

        @pl.when(z < A - 1)
        def _():
            sweep_r(k).start()

    def st_sweep_l(k):
        @pl.when(z == A - 1)
        def _():
            lout[k] = t2[k]

        @pl.when((z > 0) & (z < A - 1))
        def _():
            sweep_l(k).wait_recv()
            lout[k] = t2[k] + lin[k]

        @pl.when(z > 0)
        def _():
            sweep_l(k).start()

    def st_yag(k):
        @pl.when(z == 0)
        def _():
            sweep_l(k).wait_recv()
            full[k, frows(y), :] = t2[k] + lin[k]

        @pl.when(z == A - 1)
        def _():
            sweep_r(k).wait_recv()
            full[k, frows(y), :] = t2[k] + rin[k]

        @pl.when((z > 0) & (z < A - 1))
        def _():
            full[k, frows(y), :] = rout[k] + lin[k]

        for d in range(1, B):
            y_ag(k, d).start()

    def st_cag(k):
        for d in range(1, B):
            y_ag_in(k, d).wait_recv()
        c_ag(k).start()

    def st_chain_r(k):
        for d in range(1, A):
            cut = slice(d * ZP, (d + 1) * ZP)

            @pl.when((z < d) & (z == 0))
            def _():
                zr_out[k, :, cut] = t1[k, :, cut]

            @pl.when((z < d) & (z > 0))
            def _():
                chain_r(k, d).wait_recv()
                zr_out[k, :, cut] = t1[k, :, cut] + zr_in[k, :, cut]

            @pl.when(z < d)
            def _():
                chain_r(k, d).start()

    def st_chain_l(k):
        for d in range(A - 1):
            cut = slice(d * ZP, (d + 1) * ZP)

            @pl.when((z > d) & (z == A - 1))
            def _():
                zl_out[k, :, cut] = t1[k, :, cut]

            @pl.when((z > d) & (z < A - 1))
            def _():
                chain_l(k, d).wait_recv()
                zl_out[k, :, cut] = t1[k, :, cut] + zl_in[k, :, cut]

            @pl.when(z > d)
            def _():
                chain_l(k, d).start()

    def st_zy(k):
        for d in range(A):
            cut = slice(d * ZP, (d + 1) * ZP)

            @pl.when(z == d)
            def _():
                total = t1[k, :, cut]
                if d > 0:
                    chain_r(k, d).wait_recv()
                    total = total + zr_in[k, :, cut]
                if d < A - 1:
                    chain_l(k, d).wait_recv()
                    total = total + zl_in[k, :, cut]
                zy_out[k] = total

        for d in range(1, B):
            z_y(k, d).start()

    def st_zysum(k):
        total = zy_out[k]
        for d in range(1, B):
            z_y(k, d).wait_recv()
            total = total + zy_in[k, d - 1]
        full[k, pl.ds(hrow, HV), lanes(z)] = total

    def gather_in(k, j):
        @pl.when(z - j >= 0)
        def _():
            gather_r(k, j, lax.rem(z - j + A, A)).wait_recv()

        @pl.when(z + j < A)
        def _():
            gather_l(k, j, lax.rem(z + j, A)).wait_recv()

    def gather_out(k, j):
        @pl.when((z - j + 1 >= 0) & (z < A - 1))
        def _():
            gather_r(k, j, lax.rem(z - j + 1 + A, A)).start()

        @pl.when((z + j - 1 < A) & (z > 0))
        def _():
            gather_l(k, j, lax.rem(z + j - 1, A)).start()

    def st_gather(j, k):
        if j > 1:
            gather_in(k, j - 1)
        gather_out(k, j)

    def st_zcag(k):
        gather_in(k, A - 1)
        c_ag(k).start()

    def st_comp(k):
        c_ag_in(k).wait_recv()
        source = full[k]
        for l in range(O):
            ints = lax.dot_general(
                source, f_ref[l], (((1,), (1,)), ((), ())), preferred_element_type=F32
            )
            top = 2.0 * ints - jnp.transpose(ints)
            den = (occ_ref[plan_ref[k]] + eloc[l][:, :1]) - vsum[...]
            code = lax.rem(k, SRC) * O + l
            hits = jnp.where(pairs_ref[pl.ds(k // SRC, 1), :] == code, 1.0, 0.0)
            listed = jnp.max(hits, axis=1, keepdims=True)
            wbuf[:, l * V:(l + 1) * V] = (top / den * listed).astype(BF)
        gamma = jnp.dot(
            wbuf[...], f_ref[...].reshape(O * V, NP), preferred_element_type=F32
        )
        gsum[k] = gamma.reshape(A, B, 2, R, NP)
        gc_out[k] = gsum[k, :, :, 1 - h].astype(BF)
        g_core(k).start()

    def st_gy(k):
        g_core(k).wait_recv()
        gmid[k] = gsum[k, :, :, h] + gc_in[k].astype(F32)
        for d in range(1, B):
            gy_out[k, d - 1] = gmid[k, :, ypeer(d)].astype(BF)
            g_y(k, d).start()

    def st_gz(k):
        for d in range(1, B):
            g_y(k, d).wait_recv()
            gmid[k, :, y] = gmid[k, :, y] + gy_in[k, d - 1].astype(F32)
        for d in range(1, A):
            gz_out[k, d - 1] = gmid[k, zpeer(d), y].astype(BF)
            g_z(k, d).start()

    def st_gend(k):
        total = gmid[k, z, y]
        for d in range(1, A):
            g_z(k, d).wait_recv()
            total = total + gz_in[k, d - 1].astype(F32)
        acc[k] = total

    def z_first(k):
        return (lax.rem(k, 2) == 0) & (2 * k < K)

    vrow = jnp.broadcast_to(vrow_ref[...], (V, V))
    vsum[...] = vrow + jnp.transpose(vrow)
    for l in range(O):
        mine = jnp.where(slots_ref[...] == col * O + l, occs_ref[...], 0.0)
        eloc[l] = jnp.broadcast_to(jnp.sum(mine, axis=1, keepdims=True), (1, 128))

    def tick(t, carry):
        def run(delay, stage, kind):
            k = t - delay
            kept = (k >= 0) & (k < K)
            if kind == "z":
                kept = kept & z_first(k)
            if kind == "y":
                kept = kept & jnp.logical_not(z_first(k))
            pl.when(kept)(partial(stage, k))

        mirror = A - 1 - z
        run(0, st_core, "")
        run(1, st_half, "")
        run(1, y_send, "y")
        run(1 + z, st_chain_r, "z")
        run(1 + mirror, st_chain_l, "z")
        run(2, y_sum, "y")
        run(2 + z, st_sweep_r, "y")
        run(2 + mirror, st_sweep_l, "y")
        run(A, st_zy, "z")
        run(A + 1, st_yag, "y")
        run(A + 1, st_zysum, "z")
        for j in range(1, A):
            run(A + j, partial(st_gather, j), "z")
        run(2 * A, st_zcag, "z")
        run(A + 2, st_cag, "y")
        y_comp, z_comp = A + 3, 2 * A + 1
        for comp, kind in ((y_comp, "y"), (z_comp, "z")):
            run(comp + 3, st_gend, kind)
            run(comp + 2, st_gz, kind)
            run(comp + 1, st_gy, kind)
            run(comp, st_comp, kind)

        @pl.when(t == 2)
        def _():
            for d in range(1, NR):
                m_copy(d).start()

        return carry

    lax.fori_loop(0, K + 2 * A + 4, tick, 0)

    m_local.wait()
    for d in range(1, NR):
        m_copy(d).wait()
    root = mroot[...].reshape(NP, NP)
    gamma = acc[...].reshape(K * R, NP)
    high = gamma.astype(BF)
    low = (gamma - high.astype(F32)).astype(BF)
    fitted = jnp.dot(high, root, preferred_element_type=F32)
    fitted = fitted + jnp.dot(low, root, preferred_element_type=F32)
    out_ref[...] = fitted.reshape(K, R, NP)

    def drain(k, carry):
        core_rs(k).wait_send()
        for d in range(1, B):
            g_y(k, d).wait_send()
        for d in range(1, A):
            g_z(k, d).wait_send()
        c_ag(k).wait_send()
        g_core(k).wait_send()

        @pl.when(jnp.logical_not(z_first(k)))
        def _():
            for d in range(1, B):
                y_rs(k, d).wait_send()
                y_ag(k, d).wait_send()
            pl.when(z < A - 1)(lambda: sweep_r(k).wait_send())
            pl.when(z > 0)(lambda: sweep_l(k).wait_send())

        @pl.when(z_first(k))
        def _():
            for d in range(1, B):
                z_y(k, d).wait_send()
            for d in range(A):
                pl.when(z < d)(lambda: chain_r(k, d).wait_send())
                pl.when(z > d)(lambda: chain_l(k, d).wait_send())
            for j in range(1, A):
                pl.when((z - j + 1 >= 0) & (z < A - 1))(
                    lambda: gather_r(k, j, lax.rem(z - j + 1 + A, A)).wait_send()
                )
                pl.when((z + j - 1 < A) & (z > 0))(
                    lambda: gather_l(k, j, lax.rem(z + j - 1, A)).wait_send()
                )

        return carry

    lax.fori_loop(0, K, drain, 0)


def on_device(factors, metric_root, occ_energy, vir_energy, orbital_slot, source_plan, pair_list):
    O, V, NP = factors.shape
    n = lax.axis_size("col")
    NR = lax.axis_size("row")
    chips = n // 2
    A = 4 if chips % 4 == 0 else chips
    B = chips // A
    steps, sources = source_plan.shape[1:]
    K = steps * sources
    R = V // n
    HV, YV, ZP = V // 2, V // 2 // B, NP // A
    dma = pltpu.SemaphoreType.DMA
    b1, a1 = max(B - 1, 1), max(A - 1, 1)
    per_k = (K,)
    sems = []
    for shape in (
        per_k, (K, b1), per_k, per_k, (K, A), (K, A), (K, b1), (K, a1), (K, a1),
        (K, b1), per_k, per_k, (K, b1), (K, a1),
    ):
        sems += [dma(shape), dma(shape)]
    nr1 = max(NR - 1, 1)
    sems += [dma((nr1,)), dma((nr1,)), dma]
    vm = pltpu.VMEM
    out = pl.pallas_call(
        partial(kernel, (K, A, B, NR, O, V, NP, sources)),
        out_shape=jax.ShapeDtypeStruct((K, R, NP), F32),
        in_specs=[pl.BlockSpec(memory_space=pltpu.SMEM)] * 3 + [pl.BlockSpec(memory_space=vm)] * 6,
        out_specs=pl.BlockSpec(memory_space=vm),
        scratch_shapes=[
            vm((K, HV, NP), BF),
            vm((K, HV, NP), BF),
            vm((K, HV, NP), BF),
            vm((K, b1, YV, NP), BF),
            vm((K, YV, NP), BF),
            vm((K, YV, NP), BF),
            vm((K, YV, NP), BF),
            vm((K, YV, NP), BF),
            vm((K, YV, NP), BF),
            vm((K, HV, NP), BF),
            vm((K, HV, NP), BF),
            vm((K, HV, NP), BF),
            vm((K, HV, NP), BF),
            vm((K, HV, ZP), BF),
            vm((K, b1, HV, ZP), BF),
            vm((K, V, NP), BF),
            vm((V, V), F32),
            vm((O, 1, 128), F32),
            vm((V, O * V), BF),
            vm((K, A, B, 2, R, NP), F32),
            vm((K, A, B, R, NP), BF),
            vm((K, A, B, R, NP), BF),
            vm((K, A, B, R, NP), F32),
            vm((K, b1, A, R, NP), BF),
            vm((K, b1, A, R, NP), BF),
            vm((K, a1, R, NP), BF),
            vm((K, a1, R, NP), BF),
            vm((K, R, NP), F32),
            vm((NR, NP // NR, NP), BF),
        ] + sems,
        compiler_params=pltpu.CompilerParams(
            collective_id=0, has_side_effects=True, vmem_limit_bytes=60 * 1024 * 1024
        ),
    )(
        source_plan.reshape(K), orbital_slot, occ_energy,
        factors, metric_root, vir_energy[None, :], orbital_slot[None, :], occ_energy[None, :],
        pair_list.reshape(steps, -1),
    )
    return jnp.transpose(out, (1, 0, 2))[None]


def solution(mesh):
    in_specs = (
        P("col", None, None),
        P("row", None),
        P(),
        P(),
        P(),
        P("row", None, None),
        P("row", "col", None, None),
    )
    out_specs = P("row", "col", None, None)
    return jax.shard_map(
        on_device, mesh=mesh, in_specs=in_specs, out_specs=out_specs, check_vma=False
    )
```
